32 devices in a mesh: ctx: 2 (over y), fsdp: 4 (over z), rep: 4 (over x, core).
Axes of the slice: x: 2, y: 2, z: 4, core: 2. Of those that a mesh axis runs over, the one named last changes fastest.
Arguments:
- tokens: bfloat16 [16, 256, 2048], P(('fsdp', 'rep'), 'ctx'), may hold values from -6 to 6
- cotangent: bfloat16 [16, 256, 2048], P(('fsdp', 'rep'), 'ctx'), may hold values from -6 to 6
- lengths: int32 [16], P(('fsdp', 'rep')), may hold values from 64 to 256, as said below
- first_gain: bfloat16 [2048], P('fsdp'), may hold values from 0.25 to 1.75
- joint_matrix: bfloat16 [2048, 1920], P('fsdp'), may hold values from -0.125 to 0.125
- query_gain: bfloat16 [64], P('fsdp'), may hold values from 0.25 to 1.75
- key_gain: bfloat16 [64], P('fsdp'), may hold values from 0.25 to 1.75
- out_weight: bfloat16 [1280, 2048], P('fsdp'), may hold values from -2 to 2
- second_gain: bfloat16 [2048], P('fsdp'), may hold values from 0.25 to 1.75
- expand_weight: bfloat16 [2048, 10240], P('fsdp'), may hold values from -0.125 to 0.125
- contract_weight: bfloat16 [5120, 2048], P('fsdp'), may hold values from -0.078125 to 0.078125
Outputs:
- layer_output: bfloat16 [16, 256, 2048], P(('fsdp', 'rep'), 'ctx')
- input_gradient: float32 [16, 256, 2048], P(('fsdp', 'rep'), 'ctx')
- first_gradient: float32 [2048], P('fsdp')
- joint_gradient: float32 [2048, 1920], P('fsdp')
- query_gradient: float32 [64], P('fsdp')
- key_gradient: float32 [64], P('fsdp')
- out_gradient: float32 [1280, 2048], P('fsdp')
- second_gradient: float32 [2048], P('fsdp')
- expand_gradient: float32 [2048, 10240], P('fsdp')
- contract_gradient: float32 [5120, 2048], P('fsdp')
The draws below stay inside these ranges and needn't reach their ends.
Inputs may be any that keep to these rules, and one draw needn't show every extreme that they name: `lengths`: valid positions count from each slot's start; some slot is full and some slot has 64.
All inputs are finite; a program needn't handle non-finite values.
Results may differ from the reference program's by a relative error of at most 0.012.
Values may be sent and summed in bfloat16 or wider, within the bound.
No kernel may reach another device: no remote copies, remote signals or barrier semaphores. Data moves between devices by JAX's collectives and lax.ppermute only.
A program may use at most 384 MiB of HBM per device.

```python
import math
import jax
import jax.numpy as jnp
from jax import lax

MODEL_WIDTH = 2048
QUERY_HEADS = 20
KEY_VALUE_HEADS = 5
HEAD_SIZE = 64
FF = 5120
SLOT_LENGTH = 256
SLOTS = 16


def draw_lengths(key, part):
    value_rows = jax.random.randint(key, (SLOTS,), SLOT_LENGTH // 4, SLOT_LENGTH + 1)
    value_rows = value_rows.at[0].set(SLOT_LENGTH)
    value_rows = value_rows.at[1].set(SLOT_LENGTH // 4)
    return value_rows.astype(jnp.int32)


def block_scale(key, shape, shards, smallest, top_value):
    level, own = 1.0, jax.random.fold_in(key, 6)
    for position, parts in shards:
        draws = jnp.exp(jax.random.uniform(jax.random.fold_in(own, position), (parts,), jnp.float32, smallest / len(shards), top_value / len(shards)))
        level = level * jnp.repeat(draws, shape[position] // parts).reshape([-1 if axis == position else 1 for axis in range(len(shape))])
    return level


def gaussian(rng, extent, scale, most, shards=(), kind=jnp.bfloat16):
    array = scale * jax.random.normal(rng, extent, jnp.float32)
    if shards:
        array = array * block_scale(rng, extent, shards, -0.22, 0.18)
    return jnp.clip(array, -most, most).astype(kind)


def setup_inputs(seed: int = 0) -> dict:
    keys = jax.random.split(jax.random.key(seed), 12)
    return {
        "tokens": gaussian(keys[0], (SLOTS, SLOT_LENGTH, MODEL_WIDTH), 1.0, 6.0, ((0, 16), (1, 2))),
        "cotangent": gaussian(keys[1], (SLOTS, SLOT_LENGTH, MODEL_WIDTH), 1.0, 6.0, ((0, 16), (1, 2))),
        "lengths": draw_lengths(jax.random.fold_in(keys[11], 71), 0),
        "first_gain": jnp.clip(1.0 + 0.15 * jax.random.normal(keys[3], (MODEL_WIDTH,), jnp.float32), 0.25, 1.75).astype(jnp.bfloat16),
        "joint_matrix": gaussian(keys[4], (MODEL_WIDTH, (QUERY_HEADS + 2 * KEY_VALUE_HEADS) * HEAD_SIZE), MODEL_WIDTH ** -0.5, 0.125, ((0, 4),)),
        "query_gain": jnp.clip(1.0 + 0.15 * jax.random.normal(keys[5], (HEAD_SIZE,), jnp.float32), 0.25, 1.75).astype(jnp.bfloat16),
        "key_gain": jnp.clip(1.0 + 0.15 * jax.random.normal(keys[6], (HEAD_SIZE,), jnp.float32), 0.25, 1.75).astype(jnp.bfloat16),
        "out_weight": gaussian(keys[7], (QUERY_HEADS * HEAD_SIZE, MODEL_WIDTH), (max(1, QUERY_HEADS * HEAD_SIZE // 128)) ** -0.5, 2.0, ((0, 4),)),
        "second_gain": jnp.clip(1.0 + 0.15 * jax.random.normal(keys[8], (MODEL_WIDTH,), jnp.float32), 0.25, 1.75).astype(jnp.bfloat16),
        "expand_weight": gaussian(keys[9], (MODEL_WIDTH, 2 * FF), MODEL_WIDTH ** -0.5, 0.125, ((0, 4),)),
        "contract_weight": gaussian(keys[10], (FF, MODEL_WIDTH), FF ** -0.5, 0.078125, ((0, 4),)),
    }


@jax.custom_vjp
def lower_bound(v):
    return lax.optimization_barrier(v.astype(jnp.bfloat16)).astype(jnp.float32)

@jax.custom_vjp
def lower_backward(v):
    return v

def low_keep(v):
    return (lower_bound(v), None)

def low_pass(kept, grad):
    return (grad,)

def back_keep(v):
    return (v, None)

def back_low(kept, grad):
    return (lower_bound(grad),)
lower_bound.defvjp(low_keep, low_pass)
lower_backward.defvjp(back_keep, back_low)
epsilon = 1e-06
precise = lax.Precision.HIGHEST

def tables(positions, width):
    steps = jnp.arange(width // 2, dtype=jnp.float32)
    rates = jnp.exp(steps * (-2.0 * math.log(10000.0) / width))
    angles = positions.astype(jnp.float32)[:, None] * rates[None, :]
    return (jnp.cos(angles)[:, None, :], jnp.sin(angles)[:, None, :])

def rotate(field, cosine_table, sine_table):
    half = field.shape[-1] // 2
    first, second = (field[..., :half], field[..., half:])
    return jnp.concatenate([first * cosine_table - second * sine_table, second * cosine_table + first * sine_table], axis=-1)

def rms_scale(field, gain):
    return field * lax.rsqrt(lax.optimization_barrier(jnp.mean(field * field, axis=-1, keepdims=True)) + epsilon) * gain

def attend_block(query_rows, key_rows, value_rows, slot_length_value):
    block = min(512, SLOT_LENGTH)
    count = SLOT_LENGTH // block
    positions = jnp.arange(SLOT_LENGTH, dtype=jnp.int32)

    def one_block(index):
        rows = lax.dynamic_slice_in_dim(query_rows, index * block, block, 0)
        row_pos = index * block + jnp.arange(block, dtype=jnp.int32)
        scores = jnp.einsum('qgrd,kgd->grqk', rows, key_rows, precision=precise) * HEAD_SIZE ** (-0.5)
        scores = lower_backward(scores)
        allowed = (positions[None, :] <= row_pos[:, None]) & (positions[None, :] < slot_length_value)
        scores = jnp.where(allowed, scores, -1e+30)
        shares = lower_bound(jax.nn.softmax(scores, axis=-1))
        return jnp.einsum('grqk,kgd->qgrd', shares, value_rows, precision=precise)
    blocks = lax.map(jax.checkpoint(one_block), jnp.arange(count, dtype=jnp.int32))
    return blocks.reshape(SLOT_LENGTH, QUERY_HEADS * HEAD_SIZE)

def layer(tokens, first_gain, joint_matrix, query_gain, key_gain, out_weight, second_gain, expand_weight, contract_weight, slot_length_value):
    positions = jnp.arange(SLOT_LENGTH, dtype=jnp.int32)
    valid = (positions < slot_length_value).astype(jnp.float32)[:, None]
    entry_one = lower_bound(rms_scale(tokens, first_gain))
    joint_projection = lower_backward(jnp.dot(entry_one, joint_matrix, precision=precise))
    query_span_width = QUERY_HEADS * HEAD_SIZE
    key_span_width = KEY_VALUE_HEADS * HEAD_SIZE
    query_rows = joint_projection[:, :query_span_width].reshape(SLOT_LENGTH, QUERY_HEADS, HEAD_SIZE)
    key_rows = joint_projection[:, query_span_width:query_span_width + key_span_width].reshape(SLOT_LENGTH, KEY_VALUE_HEADS, HEAD_SIZE)
    value_rows = lower_bound(joint_projection[:, query_span_width + key_span_width:].reshape(SLOT_LENGTH, KEY_VALUE_HEADS, HEAD_SIZE))
    cosine_table, sine_table = tables(positions, HEAD_SIZE)
    query_rows = lower_bound(rotate(rms_scale(query_rows, query_gain), cosine_table, sine_table))
    key_rows = lower_bound(rotate(rms_scale(key_rows, key_gain), cosine_table, sine_table))
    mixed_output = lower_backward(lower_bound(attend_block(query_rows.reshape(SLOT_LENGTH, KEY_VALUE_HEADS, QUERY_HEADS // KEY_VALUE_HEADS, HEAD_SIZE), key_rows, value_rows, slot_length_value)))
    branch = lower_backward(jnp.dot(mixed_output, out_weight, precision=precise))
    hidden = tokens + branch
    entry_two = lower_bound(rms_scale(hidden, second_gain))
    expanded = lower_backward(jnp.dot(entry_two, expand_weight, precision=precise))
    gate, upward = (expanded[:, :FF], expanded[:, FF:])
    product = lower_bound(jax.nn.silu(gate) * upward)
    branch_two = lower_backward(jnp.dot(product, contract_weight, precision=precise))
    return (hidden + branch_two) * valid

def reference(tokens, cotangent, lengths, first_gain, joint_matrix, query_gain, key_gain, out_weight, second_gain, expand_weight, contract_weight):
    weights = tuple((w.astype(jnp.float32) for w in (first_gain, joint_matrix, query_gain, key_gain, out_weight, second_gain, expand_weight, contract_weight)))

    def per_slot(totals, items):
        slot_tokens, slot_cotangent, slot_length_value = items

        def forward(rows, *params):
            return layer(rows, *params, slot_length_value)
        result, pullback = jax.vjp(forward, slot_tokens.astype(jnp.float32), *weights)
        gradients = pullback(slot_cotangent.astype(jnp.float32))
        totals = tuple((t + g for t, g in zip(totals, gradients[1:])))
        return (totals, (result.astype(jnp.bfloat16), gradients[0]))
    zero_filled = tuple((jnp.zeros_like(w) for w in weights))
    totals, (outputs, input_gradient) = lax.scan(per_slot, zero_filled, (tokens, cotangent, lengths))
    return (outputs, input_gradient) + tuple(totals)
```

```python
import functools
import math

import jax
import jax.numpy as jnp
from jax import lax
from jax.experimental import pallas as pl
from jax.experimental.pallas import tpu as pltpu
from jax.sharding import PartitionSpec as P

QUERY_HEADS = 20
KEY_VALUE_HEADS = 5
HEAD_SIZE = 64
FF = 5120
LANES = 128

epsilon = 1e-06
masked_fill_value = -1e30
PLANE = ("ctx", "rep")
BF = jnp.bfloat16
F32 = jnp.float32


def tables(positions, width):
    steps = jnp.arange(width // 2, dtype=jnp.float32)
    rates = jnp.exp(steps * (-2.0 * math.log(10000.0) / width))
    angles = positions.astype(jnp.float32)[:, None] * rates[None, :]
    return (jnp.cos(angles)[:, None, :], jnp.sin(angles)[:, None, :])


def rotate(field, cosine_table, sine_table):
    half = field.shape[-1] // 2
    first, second = (field[..., :half], field[..., half:])
    return jnp.concatenate(
        [first * cosine_table - second * sine_table, second * cosine_table + first * sine_table],
        axis=-1,
    )


def reverse_rotation(upstream, cosine_table, sine_table):
    half = upstream.shape[-1] // 2
    first, second = (upstream[..., :half], upstream[..., half:])
    return jnp.concatenate(
        [first * cosine_table + second * sine_table, second * cosine_table - first * sine_table],
        axis=-1,
    )


def rms_parts(field):
    inverse = lax.rsqrt(jnp.mean(field * field, axis=-1, keepdims=True) + epsilon)
    return (field * inverse, inverse)


def rms_back(upstream, normed, inverse):
    return inverse * (upstream - normed * jnp.mean(upstream * normed, axis=-1, keepdims=True))


def dot(left, right, dims, out=F32):
    got = lax.dot_general(left, right, (dims, ((), ())), preferred_element_type=F32)
    return got.astype(out)


def cross_product(left, right, out=F32):
    return dot(left, right, ((0,), (0,)), out)


def against(left, right, out=F32):
    return dot(left, right, ((1,), (1,)), out)


class Plane:
    def __init__(self):
        self.c, self.r, self.z = (lax.axis_size(a) for a in ("ctx", "rep", "fsdp"))
        self.size = self.c * self.r
        self.cube = self.c == 2 and self.r == 4
        self.y = lax.axis_index("ctx")
        rep = lax.axis_index("rep")
        self.x, self.core = rep // 2, rep % 2
        self.rank = self.y * self.r + rep
        self.layer = lax.axis_index("fsdp")

    def over_x(self, v):
        return lax.ppermute(v, "rep", [(i, i ^ 2) for i in range(4)])

    def over_core(self, v):
        return lax.ppermute(v, "rep", [(i, i ^ 1) for i in range(4)])

    def over_y(self, v):
        return lax.ppermute(v, "ctx", [(0, 1), (1, 0)])

    def gather(self, v, axis=0):
        if not self.cube:
            return lax.all_gather(v, PLANE, axis=axis, tiled=False)
        half = v.shape[0] // 2
        from_x, from_y = self.over_x(v), self.over_y(v)
        far_a = self.over_y(from_x[:half])
        far_b = self.over_x(from_y[half:])
        far = jnp.concatenate([far_a, far_b], axis=0)
        x, y = self.x, self.y
        near = place(
            [(v, 2 * y + x), (from_x, 2 * y + 1 - x), (from_y, 2 * (1 - y) + x), (far, 2 * (1 - y) + 1 - x)],
            4,
            axis,
        )
        other = self.over_core(near)
        both = place([(near, self.core), (other, 1 - self.core)], 2, axis + 1)
        return both.reshape(both.shape[:axis] + (8,) + both.shape[axis + 2 :])

    def scatter(self, v, axis=0):
        if not self.cube:
            moved = jnp.moveaxis(v, axis, 0)
            return lax.psum_scatter(moved.astype(BF), PLANE, scatter_dimension=0, tiled=False).astype(F32)
        v = v.reshape(v.shape[:axis] + (2, 2, 2) + v.shape[axis + 1 :])
        pick = lambda a, i, ax: lax.dynamic_index_in_dim(a, i, ax, keepdims=False)
        x, y, core = self.x, self.y, self.core
        got = self.over_core(pick(v, 1 - core, axis + 2).astype(BF))
        v = pick(v, core, axis + 2).astype(F32) + got.astype(F32)
        row, away = pick(v, y, axis), pick(v, 1 - y, axis)
        far = pick(away, 1 - x, axis).astype(BF)
        near_y, near_x, mine = pick(away, x, axis), pick(row, 1 - x, axis), pick(row, x, axis)
        half = far.shape[0] // 2
        got_x, got_y = self.over_x(far[:half]), self.over_y(far[half:])
        near_y = jnp.concatenate([near_y[:half] + got_x.astype(F32), near_y[half:]], axis=0)
        near_x = jnp.concatenate([near_x[:half], near_x[half:] + got_y.astype(F32)], axis=0)
        in_x, in_y = self.over_x(near_x.astype(BF)), self.over_y(near_y.astype(BF))
        return mine + in_x.astype(F32) + in_y.astype(F32)

    def layers_gather(self, v):
        z = self.z
        parts = [(v, self.layer)]
        for d in range(1, z):
            got = lax.ppermute(v, "fsdp", [(i, (i + d) % z) for i in range(z)])
            parts.append((got, (self.layer - d) % z))
        return place(parts, z, 0)

    def layers_scatter(self, v):
        z = self.z
        total = lax.dynamic_index_in_dim(v, self.layer, 0, keepdims=False).astype(F32)
        for d in range(1, z):
            out = lax.dynamic_index_in_dim(v, (self.layer + d) % z, 0, keepdims=False).astype(BF)
            total = total + lax.ppermute(out, "fsdp", [(i, (i + d) % z) for i in range(z)]).astype(F32)
        return total


def place(parts, count, axis):
    first = parts[0][0]
    shape = first.shape[:axis] + (count,) + first.shape[axis:]
    total = jnp.zeros(shape, first.dtype)
    for part, index in parts:
        total = lax.dynamic_update_index_in_dim(total, jnp.expand_dims(part, axis), index, axis)
    return total


def column_slices(matrix, rank, groups, width):
    rows, columns = matrix.shape
    span = columns // groups
    last = columns // LANES - 1
    block = min(128, rows)
    window = -(-(LANES - 1 + width) // LANES)
    if width % 32 == 0:
        window = -(-(LANES - 32 + width) // LANES)

    def body(rank_ref, *refs):
        out = refs[-1]
        for g in range(groups):
            parts = [refs[g * window + w][...].astype(F32) for w in range(window)]
            wide = jnp.concatenate(parts, axis=1)
            shift = (g * span + rank_ref[0] * width) % LANES
            wide = pltpu.roll(wide, (window * LANES - shift) % (window * LANES), 1)
            out[:, g * width : (g + 1) * width] = wide[:, :width].astype(out.dtype)

    def spec(g, w):
        def index(i, rank_ref):
            return (i, jnp.minimum((g * span + rank_ref[0] * width) // LANES + w, last))

        return pl.BlockSpec((block, LANES), index)

    return pl.pallas_call(
        body,
        out_shape=jax.ShapeDtypeStruct((rows, groups * width), matrix.dtype),
        grid_spec=pltpu.PrefetchScalarGridSpec(
            num_scalar_prefetch=1,
            grid=(rows // block,),
            in_specs=[spec(g, w) for g in range(groups) for w in range(window)],
            out_specs=pl.BlockSpec((block, groups * width), lambda i, rank_ref: (i, 0)),
        ),
        name="column_slices",
    )(rank[None].astype(jnp.int32), *([matrix] * (groups * window)))


def column_merge(parts, groups):
    ranks, rows, columns = parts.shape
    width = columns // groups
    block = 32

    def body(part_ref, out):
        for g in range(groups):
            pieces = [part_ref[k, :, g * width : (g + 1) * width].astype(F32) for k in range(ranks)]
            out[:, g * ranks * width : (g + 1) * ranks * width] = jnp.concatenate(pieces, axis=1)

    return pl.pallas_call(
        body,
        out_shape=jax.ShapeDtypeStruct((rows, ranks * columns), F32),
        grid=(rows // block,),
        in_specs=[pl.BlockSpec((ranks, block, columns), lambda i: (0, i, 0))],
        out_specs=pl.BlockSpec((block, ranks * columns), lambda i: (i, 0)),
        name="column_merge",
    )(parts)


def shards(
    tokens,
    cotangent,
    lengths,
    first_gain,
    joint_matrix,
    query_gain,
    key_gain,
    out_weight,
    second_gain,
    expand_weight,
    contract_weight,
):
    plane = Plane()
    members, layers, rank = plane.size, plane.z, plane.rank
    rows_here = tokens.shape[1]
    model = tokens.shape[2]
    place_ctx = lax.axis_index("ctx")
    contexts = lax.axis_size("ctx")
    span = rows_here * contexts
    slot_length_value = lengths[0]
    positions = place_ctx * rows_here + jnp.arange(rows_here, dtype=jnp.int32)
    valid = (positions < slot_length_value).astype(F32)[:, None]
    query_width = QUERY_HEADS * HEAD_SIZE
    key_width = KEY_VALUE_HEADS * HEAD_SIZE
    head_group = QUERY_HEADS // KEY_VALUE_HEADS
    scale = HEAD_SIZE ** (-0.5)
    joint_columns = joint_matrix.shape[1]

    sizes = [first_gain.shape[0], second_gain.shape[0], query_gain.shape[0], key_gain.shape[0]]
    packed = plane.layers_gather(jnp.concatenate([first_gain, second_gain, query_gain, key_gain]))
    gains, at = [], 0
    for size in sizes:
        gains.append(packed[:, at : at + size].reshape(-1).astype(F32))
        at += size
    gain_one, gain_two, query_scale, key_scale = gains

    joint_rows = joint_matrix.shape[0] // members
    out_rows = out_weight.shape[0] // members
    joint_share = plane.layers_gather(lax.dynamic_slice_in_dim(joint_matrix, rank * joint_rows, joint_rows, 0))
    joint_full = plane.gather(joint_share, axis=1).reshape(model, joint_columns)
    out_share = plane.layers_gather(lax.dynamic_slice_in_dim(out_weight, rank * out_rows, out_rows, 0))
    out_full = plane.gather(out_share, axis=1).reshape(query_width, model)

    units = contract_weight.shape[0] // members
    expand_share = column_slices(expand_weight, rank, 2 * layers, units)
    expand_part = lax.all_gather(expand_share, "fsdp", axis=0, tiled=True)
    contract_share = lax.dynamic_slice_in_dim(contract_weight, rank * units, units, 0)
    contract_part = lax.all_gather(contract_share, "fsdp", axis=0, tiled=True)
    width = units * layers

    upstream = cotangent[0].astype(F32) * valid
    upstream_all = plane.gather(upstream.astype(BF)).reshape(members * rows_here, model)

    rows = tokens[0].astype(F32)
    normed_one, inverse_one = rms_parts(rows)
    entry_one = (normed_one * gain_one).astype(BF)
    joint_projection = dot(entry_one, joint_full, ((1,), (0,)))
    query_raw = joint_projection[:, :query_width].reshape(rows_here, QUERY_HEADS, HEAD_SIZE)
    key_raw = joint_projection[:, query_width : query_width + key_width].reshape(
        rows_here, KEY_VALUE_HEADS, HEAD_SIZE
    )
    value_part = joint_projection[:, query_width + key_width :]
    cosine_table, sine_table = tables(positions, HEAD_SIZE)
    query_normed, query_inverse = rms_parts(query_raw)
    rotated_query = rotate(query_normed * query_scale, cosine_table, sine_table).astype(BF)
    key_normed, key_inverse = rms_parts(key_raw)
    key_rot = rotate(key_normed * key_scale, cosine_table, sine_table).astype(BF)
    local_pair = jnp.concatenate([key_rot.reshape(rows_here, key_width), value_part.astype(BF)], axis=1)
    if contexts == 2:
        earlier = lax.ppermute(local_pair, "ctx", [(0, 1)])
        first = place_ctx == 0
        pair_all = jnp.concatenate(
            [jnp.where(first, local_pair, earlier), jnp.where(first, 0, local_pair).astype(BF)], axis=0
        )
    else:
        pair_all = lax.all_gather(local_pair, "ctx", axis=0, tiled=True)
    key_all = pair_all[:, :key_width].reshape(span, KEY_VALUE_HEADS, HEAD_SIZE)
    value_all = pair_all[:, key_width:].reshape(span, KEY_VALUE_HEADS, HEAD_SIZE)
    grouped_query = rotated_query.reshape(rows_here, KEY_VALUE_HEADS, head_group, HEAD_SIZE)
    key_pos = jnp.arange(span, dtype=jnp.int32)
    allowed = (key_pos[None, :] <= positions[:, None]) & (key_pos[None, :] < slot_length_value)
    scores = jnp.einsum("qgrd,kgd->grqk", grouped_query, key_all, preferred_element_type=F32) * scale
    scores = jnp.where(allowed, scores, masked_fill_value)
    powers = jnp.where(allowed, jnp.exp(scores - jnp.max(scores, axis=-1, keepdims=True)), 0.0)
    shares = powers / jnp.sum(powers, axis=-1, keepdims=True)
    shares_b = shares.astype(BF)
    mixed = jnp.einsum("grqk,kgd->qgrd", shares_b, value_all, preferred_element_type=F32)
    mixed_output = mixed.reshape(rows_here, query_width).astype(BF)
    hidden = rows + dot(mixed_output, out_full, ((1,), (0,)))

    normed_two, inverse_two = rms_parts(hidden)
    entry_two = (normed_two * gain_two).astype(BF)
    entry_all = plane.gather(entry_two).reshape(members * rows_here, model)
    expanded = dot(entry_all, expand_part, ((1,), (0,)))
    gate, upward = expanded[:, :width], expanded[:, width:]
    sigma = jax.nn.sigmoid(gate)
    activated = gate * sigma
    product = (activated * upward).astype(BF)
    back_product = against(upstream_all, contract_part)
    grad_gate = back_product * upward * sigma * (1.0 + gate * (1.0 - sigma))
    grad_upward = back_product * activated
    grad_expanded = jnp.concatenate([grad_gate, grad_upward], axis=1).astype(BF)
    back_entry_share = against(grad_expanded, expand_part, BF)
    back_entry_two = plane.scatter(back_entry_share.reshape(members, rows_here, model))
    contract_grad = cross_product(product, upstream_all, BF)
    contract_owned = lax.psum_scatter(contract_grad, "fsdp", scatter_dimension=0, tiled=True)
    expand_grad = cross_product(entry_all, grad_expanded, BF)
    expand_owned = lax.psum_scatter(expand_grad, "fsdp", scatter_dimension=0, tiled=True)
    branch_share = dot(product, contract_part, ((1,), (0,)), BF)
    branch_two = plane.scatter(branch_share.reshape(members, rows_here, model))
    layer_output = ((hidden + branch_two) * valid).astype(BF)

    second_grad = jnp.sum(back_entry_two * normed_two, axis=0)
    back_hidden = upstream + rms_back(back_entry_two * gain_two, normed_two, inverse_two)

    back_hidden_b = back_hidden.astype(BF)
    out_grad = cross_product(mixed_output, back_hidden_b, BF)
    out_mine = plane.scatter(out_grad.reshape(layers, members, out_rows, model), axis=1)
    mixed_backward = against(back_hidden_b, out_full, BF)
    group_backward = mixed_backward.reshape(rows_here, KEY_VALUE_HEADS, head_group, HEAD_SIZE)
    back_shares = jnp.einsum("qgrd,kgd->grqk", group_backward, value_all, preferred_element_type=F32)
    offset = jnp.sum(shares * back_shares, axis=-1, keepdims=True)
    back_scores = (shares * (back_shares - offset)).astype(BF)
    grad_query = jnp.einsum("grqk,kgd->qgrd", back_scores, key_all, preferred_element_type=F32)
    grad_keys = jnp.einsum("grqk,qgrd->kgd", back_scores, grouped_query, preferred_element_type=F32) * scale
    grad_values = jnp.einsum("grqk,qgrd->kgd", shares_b, group_backward, preferred_element_type=F32)
    pair_grads = jnp.concatenate(
        [grad_keys.reshape(span, key_width), grad_values.reshape(span, key_width)], axis=1
    )
    if contexts == 2:
        later = lax.ppermute(pair_grads[:rows_here], "ctx", [(1, 0)])
        pair_mine = jnp.where(first, pair_grads[:rows_here] + later, pair_grads[rows_here:])
    else:
        pair_mine = lax.psum_scatter(pair_grads, "ctx", scatter_dimension=0, tiled=True)
    back_query_rot = reverse_rotation(
        grad_query.reshape(rows_here, QUERY_HEADS, HEAD_SIZE) * scale, cosine_table, sine_table
    )
    query_gain_grad = jnp.sum(back_query_rot * query_normed, axis=(0, 1))
    grad_query_raw = rms_back(back_query_rot * query_scale, query_normed, query_inverse)
    back_key_rot = reverse_rotation(
        pair_mine[:, :key_width].reshape(rows_here, KEY_VALUE_HEADS, HEAD_SIZE), cosine_table, sine_table
    )
    key_gain_grad = jnp.sum(back_key_rot * key_normed, axis=(0, 1))
    grad_key_raw = rms_back(back_key_rot * key_scale, key_normed, key_inverse)
    grad_joint = jnp.concatenate(
        [
            grad_query_raw.reshape(rows_here, query_width),
            grad_key_raw.reshape(rows_here, key_width),
            pair_mine[:, key_width:],
        ],
        axis=1,
    ).astype(BF)
    joint_grad = cross_product(entry_one, grad_joint, BF)
    joint_mine = plane.scatter(joint_grad.reshape(layers, members, joint_rows, joint_columns), axis=1)
    back_entry_one = against(grad_joint, joint_full)
    first_grad = jnp.sum(back_entry_one * normed_one, axis=0)
    input_gradient = back_hidden + rms_back(back_entry_one * gain_one, normed_one, inverse_one)

    out_owned = plane.layers_scatter(out_mine).astype(BF)
    joint_owned = plane.layers_scatter(joint_mine).astype(BF)
    out_gradient = plane.gather(out_owned).reshape(members * out_rows, model).astype(F32)
    joint_gradient = plane.gather(joint_owned).reshape(members * joint_rows, joint_columns).astype(F32)
    contract_gradient = plane.gather(contract_owned).reshape(members * units, model).astype(F32)
    expand_gradient = column_merge(plane.gather(expand_owned), 2 * layers)
    small = lax.psum(
        jnp.concatenate([first_grad, second_grad, query_gain_grad, key_gain_grad]), ("ctx", "fsdp", "rep")
    )
    owned, at = [], 0
    for size in sizes:
        owned.append(lax.dynamic_slice_in_dim(small, at + plane.layer * size, size))
        at += size * layers
    return (
        layer_output[None],
        input_gradient[None],
        owned[0],
        joint_gradient,
        owned[2],
        owned[3],
        out_gradient,
        owned[1],
        expand_gradient,
        contract_gradient,
    )


def solution(mesh):
    return jax.shard_map(
        shards,
        mesh=mesh,
        in_specs=(
            P(("fsdp", "rep"), "ctx", None),
            P(("fsdp", "rep"), "ctx", None),
            P(("fsdp", "rep")),
            P("fsdp"),
            P("fsdp", None),
            P("fsdp"),
            P("fsdp"),
            P("fsdp", None),
            P("fsdp"),
            P("fsdp", None),
            P("fsdp", None),
        ),
        out_specs=(
            P(("fsdp", "rep"), "ctx", None),
            P(("fsdp", "rep"), "ctx", None),
            P("fsdp"),
            P("fsdp", None),
            P("fsdp"),
            P("fsdp"),
            P("fsdp", None),
            P("fsdp"),
            P("fsdp", None),
            P("fsdp", None),
        ),
        check_vma=False,
    )
```

```python
import functools
import math

import jax
import jax.numpy as jnp
from jax import lax
from jax.experimental import pallas as pl
from jax.experimental.pallas import tpu as pltpu
from jax.sharding import PartitionSpec as P

QUERY_HEADS = 20
KEY_VALUE_HEADS = 5
HEAD_SIZE = 64
FF = 5120
LANES = 128

epsilon = 1e-06
masked_fill_value = -1e30
PLANE = ("ctx", "rep")
BF = jnp.bfloat16
F32 = jnp.float32


def tables(positions, width):
    steps = jnp.arange(width // 2, dtype=jnp.float32)
    rates = jnp.exp(steps * (-2.0 * math.log(10000.0) / width))
    angles = positions.astype(jnp.float32)[:, None] * rates[None, :]
    return (jnp.cos(angles)[:, None, :], jnp.sin(angles)[:, None, :])


def rotate(field, cosine_table, sine_table):
    half = field.shape[-1] // 2
    first, second = (field[..., :half], field[..., half:])
    return jnp.concatenate(
        [first * cosine_table - second * sine_table, second * cosine_table + first * sine_table],
        axis=-1,
    )


def reverse_rotation(upstream, cosine_table, sine_table):
    half = upstream.shape[-1] // 2
    first, second = (upstream[..., :half], upstream[..., half:])
    return jnp.concatenate(
        [first * cosine_table + second * sine_table, second * cosine_table - first * sine_table],
        axis=-1,
    )


def rms_parts(field):
    inverse = lax.rsqrt(jnp.mean(field * field, axis=-1, keepdims=True) + epsilon)
    return (field * inverse, inverse)


def rms_back(upstream, normed, inverse):
    return inverse * (upstream - normed * jnp.mean(upstream * normed, axis=-1, keepdims=True))


def dot(left, right, dims, out=F32):
    got = lax.dot_general(left, right, (dims, ((), ())), preferred_element_type=F32)
    return got.astype(out)


def cross_product(left, right, out=F32):
    return dot(left, right, ((0,), (0,)), out)


def against(left, right, out=F32):
    return dot(left, right, ((1,), (1,)), out)


class Plane:
    def __init__(self):
        self.c, self.r, self.z = (lax.axis_size(a) for a in ("ctx", "rep", "fsdp"))
        self.size = self.c * self.r
        self.cube = self.c == 2 and self.r == 4
        self.y = lax.axis_index("ctx")
        rep = lax.axis_index("rep")
        self.x, self.core = rep // 2, rep % 2
        self.rank = self.y * self.r + rep
        self.layer = lax.axis_index("fsdp")

    def over_x(self, v):
        return lax.ppermute(v, "rep", [(i, i ^ 2) for i in range(4)])

    def over_core(self, v):
        return lax.ppermute(v, "rep", [(i, i ^ 1) for i in range(4)])

    def over_y(self, v):
        return lax.ppermute(v, "ctx", [(0, 1), (1, 0)])

    def gather(self, v, axis=0):
        if not self.cube:
            return lax.all_gather(v, PLANE, axis=axis, tiled=False)
        half = v.shape[0] // 2
        from_x, from_y = self.over_x(v), self.over_y(v)
        far_a = self.over_y(from_x[:half])
        far_b = self.over_x(from_y[half:])
        far = jnp.concatenate([far_a, far_b], axis=0)
        x, y = self.x, self.y
        near = place(
            [(v, 2 * y + x), (from_x, 2 * y + 1 - x), (from_y, 2 * (1 - y) + x), (far, 2 * (1 - y) + 1 - x)],
            4,
            axis,
        )
        other = self.over_core(near)
        both = place([(near, self.core), (other, 1 - self.core)], 2, axis + 1)
        return both.reshape(both.shape[:axis] + (8,) + both.shape[axis + 2 :])

    def scatter(self, v, axis=0):
        if not self.cube:
            moved = jnp.moveaxis(v, axis, 0)
            return lax.psum_scatter(moved.astype(BF), PLANE, scatter_dimension=0, tiled=False).astype(F32)
        v = v.reshape(v.shape[:axis] + (2, 2, 2) + v.shape[axis + 1 :])
        pick = lambda a, i, ax: lax.dynamic_index_in_dim(a, i, ax, keepdims=False)
        x, y, core = self.x, self.y, self.core
        got = self.over_core(pick(v, 1 - core, axis + 2).astype(BF))
        v = pick(v, core, axis + 2).astype(F32) + got.astype(F32)
        row, away = pick(v, y, axis), pick(v, 1 - y, axis)
        far = pick(away, 1 - x, axis).astype(BF)
        near_y, near_x, mine = pick(away, x, axis), pick(row, 1 - x, axis), pick(row, x, axis)
        half = far.shape[0] // 2
        got_x, got_y = self.over_x(far[:half]), self.over_y(far[half:])
        near_y = jnp.concatenate([near_y[:half] + got_x.astype(F32), near_y[half:]], axis=0)
        near_x = jnp.concatenate([near_x[:half], near_x[half:] + got_y.astype(F32)], axis=0)
        in_x, in_y = self.over_x(near_x.astype(BF)), self.over_y(near_y.astype(BF))
        return mine + in_x.astype(F32) + in_y.astype(F32)

    def gather_near(self, v):
        half = v.shape[0] // 2
        from_x, from_y = self.over_x(v), self.over_y(v)
        far_a = self.over_y(from_x[:half])
        far_b = self.over_x(from_y[half:])
        near = jnp.concatenate([v, from_x, from_y, far_a, far_b], axis=0)
        return near, self.over_core(near)

    def gather_rows(self, v):
        if not self.cube:
            return lax.all_gather(v, PLANE, axis=0, tiled=True)
        return jnp.concatenate(self.gather_near(v), axis=0)

    def scatter_rows(self, v):
        if not self.cube:
            return lax.psum_scatter(v.astype(BF), PLANE, scatter_dimension=0, tiled=True).astype(F32)
        n = v.shape[0] // 8
        got = self.over_core(v[4 * n :].astype(BF)).astype(F32)
        part = lambda k: v[k * n : (k + 1) * n].astype(F32) + got[k * n : (k + 1) * n]
        half = n // 2
        far = part(3).astype(BF)
        got_x, got_y = self.over_x(far[:half]), self.over_y(far[half:])
        near_x, near_y = part(1), part(2)
        near_y = jnp.concatenate([near_y[:half] + got_x.astype(F32), near_y[half:]], axis=0)
        near_x = jnp.concatenate([near_x[:half], near_x[half:] + got_y.astype(F32)], axis=0)
        in_x, in_y = self.over_x(near_x.astype(BF)), self.over_y(near_y.astype(BF))
        return part(0) + in_x.astype(F32) + in_y.astype(F32)

    def reorder(self, v):
        if not self.cube:
            return v
        n = v.shape[0] // 8
        tail = v.shape[1:]
        v = v.reshape((2, 2, 2, n) + tail)
        for axis, bit in ((0, self.y), (1, self.x), (2, self.core)):
            v = jnp.where(bit == 1, jnp.flip(v, axis), v)
        return v.reshape((8 * n,) + tail)

    def to_ranks(self, v):
        if not self.cube:
            return v
        n = v.shape[0] // 8
        v = jnp.swapaxes(v.reshape((2, 4, n) + v.shape[1:]), 0, 1).reshape(v.shape)
        return self.reorder(v)

    def from_ranks(self, v):
        if not self.cube:
            return v
        n = v.shape[0] // 8
        v = self.reorder(v)
        return jnp.swapaxes(v.reshape((4, 2, n) + v.shape[1:]), 0, 1).reshape(v.shape)

    def exchange(self, v):
        return lax.all_to_all(v, PLANE, split_axis=0, concat_axis=0, tiled=True)

    def total(self, v):
        if not self.cube:
            return lax.psum(v, ("ctx", "fsdp", "rep"))
        v = v + self.over_core(v)
        v = v + self.over_x(v)
        v = v + self.over_y(v)
        z = self.z
        parts = [lax.ppermute(v, "fsdp", [(i, (i + d) % z) for i in range(z)]) for d in range(1, z)]
        for part in parts:
            v = v + part
        return v

    def layers_gather(self, v):
        z = self.z
        parts = [(v, self.layer)]
        for d in range(1, z):
            got = lax.ppermute(v, "fsdp", [(i, (i + d) % z) for i in range(z)])
            parts.append((got, (self.layer - d) % z))
        return place(parts, z, 0)

    def layers_scatter(self, v):
        z = self.z
        total = lax.dynamic_index_in_dim(v, self.layer, 0, keepdims=False).astype(F32)
        for d in range(1, z):
            out = lax.dynamic_index_in_dim(v, (self.layer + d) % z, 0, keepdims=False).astype(BF)
            total = total + lax.ppermute(out, "fsdp", [(i, (i + d) % z) for i in range(z)]).astype(F32)
        return total


def place(parts, count, axis):
    first = parts[0][0]
    shape = first.shape[:axis] + (count,) + first.shape[axis:]
    total = jnp.zeros(shape, first.dtype)
    for part, index in parts:
        total = lax.dynamic_update_index_in_dim(total, jnp.expand_dims(part, axis), index, axis)
    return total


def column_slices(matrix, rank, groups, splits):
    rows, columns = matrix.shape
    width = sum(splits)
    span = columns // groups
    last = columns // LANES - 1
    block = min(128, rows)
    unit = math.gcd(math.gcd(width, span), LANES)
    window = -(-(LANES - unit + width) // LANES)

    def body(rank_ref, *refs):
        outs = refs[groups * window :]
        for g in range(groups):
            parts = [refs[g * window + w][...].astype(F32) for w in range(window)]
            wide = parts[0] if window == 1 else jnp.concatenate(parts, axis=1)
            shift = (g * span + rank_ref[0] * width) % LANES
            wide = pltpu.roll(wide, (window * LANES - shift) % (window * LANES), 1)
            at = 0
            for out, size in zip(outs, splits):
                out[:, g * size : (g + 1) * size] = wide[:, at : at + size].astype(out.dtype)
                at += size

    def spec(g, w):
        def index(i, rank_ref):
            return (i, jnp.minimum((g * span + rank_ref[0] * width) // LANES + w, last))

        return pl.BlockSpec((block, LANES), index)

    return pl.pallas_call(
        body,
        out_shape=[jax.ShapeDtypeStruct((rows, groups * size), matrix.dtype) for size in splits],
        grid_spec=pltpu.PrefetchScalarGridSpec(
            num_scalar_prefetch=1,
            grid=(rows // block,),
            in_specs=[spec(g, w) for g in range(groups) for w in range(window)],
            out_specs=[pl.BlockSpec((block, groups * size), lambda i, rank_ref: (i, 0)) for size in splits],
        ),
        name="column_slices",
    )(rank[None].astype(jnp.int32), *([matrix] * (groups * window)))


def column_merge(parts, groups, rank, rows):
    cube = isinstance(parts[0], tuple)
    flat = [a for part in parts for a in (part if cube else (part,))]
    sizes = [(part[0] if cube else part).shape[-1] // groups for part in parts]
    ranks = flat[0].shape[0] * (2 if cube else 1)
    span = ranks * sum(sizes)
    block = math.gcd(rows, 32)

    def body(rank_ref, *refs):
        out = refs[-1]
        core = rank_ref[0] % 2

        def load(s, k, g):
            cut = slice(g * sizes[s], (g + 1) * sizes[s])
            if not cube:
                return refs[s][k, :, cut].astype(F32)
            near, other = refs[2 * s], refs[2 * s + 1]
            index = lax.shift_right_logical(jnp.bitwise_xor(rank_ref[0], k), 1)
            mine = core == k % 2
            return jnp.where(mine, near[index, :, cut].astype(F32), other[index, :, cut].astype(F32))

        for g in range(groups):
            pieces = [load(s, k, g) for k in range(ranks) for s in range(len(sizes))]
            out[:, g * span : (g + 1) * span] = jnp.concatenate(pieces, axis=1)

    def spec(a):
        return pl.BlockSpec((a.shape[0], block, a.shape[2]), lambda i, rank_ref: (0, i, 0))

    return pl.pallas_call(
        body,
        out_shape=jax.ShapeDtypeStruct((rows, groups * span), F32),
        grid_spec=pltpu.PrefetchScalarGridSpec(
            num_scalar_prefetch=1,
            grid=(rows // block,),
            in_specs=[spec(a) for a in flat],
            out_specs=pl.BlockSpec((block, groups * span), lambda i, rank_ref: (i, 0)),
        ),
        name="column_merge",
    )(rank[None].astype(jnp.int32), *flat)


def shards(
    tokens,
    cotangent,
    lengths,
    first_gain,
    joint_matrix,
    query_gain,
    key_gain,
    out_weight,
    second_gain,
    expand_weight,
    contract_weight,
):
    plane = Plane()
    members, layers, rank = plane.size, plane.z, plane.rank
    rows_here = tokens.shape[1]
    model = tokens.shape[2]
    place_ctx = lax.axis_index("ctx")
    contexts = lax.axis_size("ctx")
    span = rows_here * contexts
    slot_length_value = lengths[0]
    positions = place_ctx * rows_here + jnp.arange(rows_here, dtype=jnp.int32)
    valid = (positions < slot_length_value).astype(F32)[:, None]
    query_width = QUERY_HEADS * HEAD_SIZE
    key_width = KEY_VALUE_HEADS * HEAD_SIZE
    head_group = QUERY_HEADS // KEY_VALUE_HEADS
    scale = HEAD_SIZE ** (-0.5)
    joint_columns = joint_matrix.shape[1]

    sizes = [first_gain.shape[0], second_gain.shape[0], query_gain.shape[0], key_gain.shape[0]]
    packed = plane.layers_gather(jnp.concatenate([first_gain, second_gain, query_gain, key_gain]))
    gains, at = [], 0
    for size in sizes:
        gains.append(packed[:, at : at + size].reshape(-1).astype(F32))
        at += size
    gain_one, gain_two, query_scale, key_scale = gains

    rows = tokens[0].astype(F32)
    tokens_all = plane.gather_rows(tokens[0])
    joint_width = joint_columns // members
    (joint_share,) = column_slices(joint_matrix, rank, 1, (joint_width,))
    joint_part = plane.layers_gather(joint_share).reshape(model, joint_width)
    out_rows = out_weight.shape[0] // members
    out_share = plane.layers_gather(lax.dynamic_slice_in_dim(out_weight, rank * out_rows, out_rows, 0))
    out_full = plane.gather(out_share, axis=1).reshape(query_width, model)

    units = contract_weight.shape[0] // members
    splits = (units * 3 // 5, units - units * 3 // 5)
    groups = 2 * layers
    expand_shares = column_slices(expand_weight, rank, groups, splits)
    parts, at = [], rank * units
    for share, size in zip(expand_shares, splits):
        contract_share = lax.dynamic_slice_in_dim(contract_weight, at, size, 0)
        at = at + size
        sent = jnp.concatenate([share, contract_share.reshape(-1, groups * size)], axis=0)
        got = lax.all_gather(sent, "fsdp", axis=0, tiled=False)
        rows_in = share.shape[0]
        parts.append((got[:, :rows_in].reshape(model, groups * size), got[:, rows_in:].reshape(size * layers, model)))

    upstream = cotangent[0].astype(F32) * valid
    upstream_all = plane.gather_rows(upstream.astype(BF))

    entry_one_all = (rms_parts(tokens_all.astype(F32))[0] * gain_one).astype(BF)
    normed_one, inverse_one = rms_parts(rows)
    joint_columns_all = plane.to_ranks(dot(entry_one_all, joint_part, ((1,), (0,)), BF))
    joint_projection = plane.exchange(joint_columns_all).reshape(members, rows_here, joint_width)
    joint_projection = jnp.swapaxes(joint_projection, 0, 1).reshape(rows_here, joint_columns).astype(F32)
    query_raw = joint_projection[:, :query_width].reshape(rows_here, QUERY_HEADS, HEAD_SIZE)
    key_raw = joint_projection[:, query_width : query_width + key_width].reshape(
        rows_here, KEY_VALUE_HEADS, HEAD_SIZE
    )
    value_part = joint_projection[:, query_width + key_width :]
    cosine_table, sine_table = tables(positions, HEAD_SIZE)
    query_normed, query_inverse = rms_parts(query_raw)
    rotated_query = rotate(query_normed * query_scale, cosine_table, sine_table).astype(BF)
    key_normed, key_inverse = rms_parts(key_raw)
    key_rot = rotate(key_normed * key_scale, cosine_table, sine_table).astype(BF)
    local_pair = jnp.concatenate([key_rot.reshape(rows_here, key_width), value_part.astype(BF)], axis=1)
    if contexts == 2:
        earlier = lax.ppermute(local_pair, "ctx", [(0, 1)])
        first = place_ctx == 0
        pair_all = jnp.concatenate(
            [jnp.where(first, local_pair, earlier), jnp.where(first, 0, local_pair).astype(BF)], axis=0
        )
    else:
        pair_all = lax.all_gather(local_pair, "ctx", axis=0, tiled=True)
    key_all = pair_all[:, :key_width].reshape(span, KEY_VALUE_HEADS, HEAD_SIZE)
    value_all = pair_all[:, key_width:].reshape(span, KEY_VALUE_HEADS, HEAD_SIZE)
    grouped_query = rotated_query.reshape(rows_here, KEY_VALUE_HEADS, head_group, HEAD_SIZE)
    key_pos = jnp.arange(span, dtype=jnp.int32)
    allowed = (key_pos[None, :] <= positions[:, None]) & (key_pos[None, :] < slot_length_value)
    scores = jnp.einsum("qgrd,kgd->grqk", grouped_query, key_all, preferred_element_type=F32) * scale
    scores = jnp.where(allowed, scores, masked_fill_value)
    powers = jnp.where(allowed, jnp.exp(scores - jnp.max(scores, axis=-1, keepdims=True)), 0.0)
    shares = powers / jnp.sum(powers, axis=-1, keepdims=True)
    shares_b = shares.astype(BF)
    mixed = jnp.einsum("grqk,kgd->qgrd", shares_b, value_all, preferred_element_type=F32)
    mixed_output = mixed.reshape(rows_here, query_width).astype(BF)
    hidden = rows + dot(mixed_output, out_full, ((1,), (0,)))

    normed_two, inverse_two = rms_parts(hidden)
    entry_two = (normed_two * gain_two).astype(BF)
    entry_all = plane.gather_rows(entry_two)
    back_entry_share = branch_share = 0.0
    reduced = []
    for size, (expand_part, contract_part) in zip(splits, parts):
        width = size * layers
        expanded = dot(entry_all, expand_part, ((1,), (0,)))
        gate, upward = expanded[:, :width], expanded[:, width:]
        sigma = jax.nn.sigmoid(gate)
        activated = gate * sigma
        product = (activated * upward).astype(BF)
        back_product = against(upstream_all, contract_part)
        grad_gate = back_product * upward * sigma * (1.0 + gate * (1.0 - sigma))
        grad_upward = back_product * activated
        grad_expanded = jnp.concatenate([grad_gate, grad_upward], axis=1).astype(BF)
        contract_grad = cross_product(product, upstream_all, BF).reshape(layers, -1, groups * size)
        expand_grad = cross_product(entry_all, grad_expanded, BF).reshape(layers, -1, groups * size)
        sent = jnp.concatenate([expand_grad, contract_grad], axis=1)
        reduced.append(lax.psum_scatter(sent, "fsdp", scatter_dimension=0, tiled=False))
        back_entry_share = back_entry_share + against(grad_expanded, expand_part)
        branch_share = branch_share + dot(product, contract_part, ((1,), (0,)))
    back_entry_two = plane.scatter_rows(back_entry_share)
    branch_two = plane.scatter_rows(branch_share)
    layer_output = ((hidden + branch_two) * valid).astype(BF)

    second_grad = jnp.sum(back_entry_two * normed_two, axis=0)
    back_hidden = upstream + rms_back(back_entry_two * gain_two, normed_two, inverse_two)

    back_hidden_b = back_hidden.astype(BF)
    out_grad = cross_product(mixed_output, back_hidden_b, BF)
    out_mine = plane.scatter(out_grad.reshape(layers, members, out_rows, model), axis=1)
    mixed_backward = against(back_hidden_b, out_full, BF)
    group_backward = mixed_backward.reshape(rows_here, KEY_VALUE_HEADS, head_group, HEAD_SIZE)
    back_shares = jnp.einsum("qgrd,kgd->grqk", group_backward, value_all, preferred_element_type=F32)
    offset = jnp.sum(shares * back_shares, axis=-1, keepdims=True)
    back_scores = (shares * (back_shares - offset)).astype(BF)
    grad_query = jnp.einsum("grqk,kgd->qgrd", back_scores, key_all, preferred_element_type=F32)
    grad_keys = jnp.einsum("grqk,qgrd->kgd", back_scores, grouped_query, preferred_element_type=F32) * scale
    grad_values = jnp.einsum("grqk,qgrd->kgd", shares_b, group_backward, preferred_element_type=F32)
    pair_grads = jnp.concatenate(
        [grad_keys.reshape(span, key_width), grad_values.reshape(span, key_width)], axis=1
    )
    if contexts == 2:
        later = lax.ppermute(pair_grads[:rows_here], "ctx", [(1, 0)])
        pair_mine = jnp.where(first, pair_grads[:rows_here] + later, pair_grads[rows_here:])
    else:
        pair_mine = lax.psum_scatter(pair_grads, "ctx", scatter_dimension=0, tiled=True)
    back_query_rot = reverse_rotation(
        grad_query.reshape(rows_here, QUERY_HEADS, HEAD_SIZE) * scale, cosine_table, sine_table
    )
    query_gain_grad = jnp.sum(back_query_rot * query_normed, axis=(0, 1))
    grad_query_raw = rms_back(back_query_rot * query_scale, query_normed, query_inverse)
    back_key_rot = reverse_rotation(
        pair_mine[:, :key_width].reshape(rows_here, KEY_VALUE_HEADS, HEAD_SIZE), cosine_table, sine_table
    )
    key_gain_grad = jnp.sum(back_key_rot * key_normed, axis=(0, 1))
    grad_key_raw = rms_back(back_key_rot * key_scale, key_normed, key_inverse)
    grad_joint = jnp.concatenate(
        [
            grad_query_raw.reshape(rows_here, query_width),
            grad_key_raw.reshape(rows_here, key_width),
            pair_mine[:, key_width:],
        ],
        axis=1,
    ).astype(BF)
    grad_joint = jnp.swapaxes(grad_joint.reshape(rows_here, members, joint_width), 0, 1)
    grad_columns = plane.from_ranks(plane.exchange(grad_joint.reshape(members * rows_here, joint_width)))
    joint_grad = cross_product(entry_one_all, grad_columns, BF).reshape(layers, -1, joint_width)
    back_entry_one = plane.scatter_rows(against(grad_columns, joint_part))
    first_grad = jnp.sum(back_entry_one * normed_one, axis=0)
    input_gradient = back_hidden + rms_back(back_entry_one * gain_one, normed_one, inverse_one)

    out_owned = plane.layers_scatter(out_mine).astype(BF)
    out_gradient = plane.gather(out_owned).reshape(members * out_rows, model).astype(F32)
    joint_owned = plane.layers_scatter(joint_grad).astype(BF)
    wide, tall = [], []
    for size, mine in zip(splits, reduced):
        rows_in = model // layers
        if plane.cube:
            halves = [h.reshape((4,) + mine.shape) for h in plane.gather_near(mine)]
            wide.append(tuple(halves))
            both = jnp.concatenate([h[:, rows_in:] for h in halves], axis=0)
        else:
            both = lax.all_gather(mine, PLANE, axis=0, tiled=False)
            wide.append(both)
            both = both[:, rows_in:]
        tall.append(plane.to_ranks(both.reshape(members * size, model)).reshape(members, size, model))
    expand_gradient = column_merge(wide, groups, rank, rows_in)
    contract_gradient = jnp.concatenate(tall, axis=1).reshape(members * units, model).astype(F32)
    if plane.cube:
        joint_pair = tuple(h.reshape((4,) + joint_owned.shape) for h in plane.gather_near(joint_owned))
        joint_gradient = column_merge([joint_pair], 1, rank, rows_in)
    else:
        joint_gradient = column_merge([lax.all_gather(joint_owned, PLANE, axis=0, tiled=False)], 1, rank, rows_in)
    small = plane.total(jnp.concatenate([first_grad, second_grad, query_gain_grad, key_gain_grad]))
    owned, at = [], 0
    for size in sizes:
        owned.append(lax.dynamic_slice_in_dim(small, at + plane.layer * size, size))
        at += size * layers
    return (
        layer_output[None],
        input_gradient[None],
        owned[0],
        joint_gradient,
        owned[2],
        owned[3],
        out_gradient,
        owned[1],
        expand_gradient,
        contract_gradient,
    )


def solution(mesh):
    return jax.shard_map(
        shards,
        mesh=mesh,
        in_specs=(
            P(("fsdp", "rep"), "ctx", None),
            P(("fsdp", "rep"), "ctx", None),
            P(("fsdp", "rep")),
            P("fsdp"),
            P("fsdp", None),
            P("fsdp"),
            P("fsdp"),
            P("fsdp", None),
            P("fsdp"),
            P("fsdp", None),
            P("fsdp", None),
        ),
        out_specs=(
            P(("fsdp", "rep"), "ctx", None),
            P(("fsdp", "rep"), "ctx", None),
            P("fsdp"),
            P("fsdp", None),
            P("fsdp"),
            P("fsdp"),
            P("fsdp", None),
            P("fsdp"),
            P("fsdp", None),
            P("fsdp", None),
        ),
        check_vma=False,
    )
```

```python
import functools
import math

import jax
import jax.numpy as jnp
from jax import lax
from jax.experimental import pallas as pl
from jax.experimental.pallas import tpu as pltpu
from jax.sharding import PartitionSpec as P

QUERY_HEADS = 20
KEY_VALUE_HEADS = 5
HEAD_SIZE = 64
FF = 5120
LANES = 128

epsilon = 1e-06
masked_fill_value = -1e30
PLANE = ("ctx", "rep")
BF = jnp.bfloat16
F32 = jnp.float32


def tables(positions, width):
    steps = jnp.arange(width // 2, dtype=jnp.float32)
    rates = jnp.exp(steps * (-2.0 * math.log(10000.0) / width))
    angles = positions.astype(jnp.float32)[:, None] * rates[None, :]
    return (jnp.cos(angles)[:, None, :], jnp.sin(angles)[:, None, :])


def rotate(field, cosine_table, sine_table):
    half = field.shape[-1] // 2
    first, second = (field[..., :half], field[..., half:])
    return jnp.concatenate(
        [first * cosine_table - second * sine_table, second * cosine_table + first * sine_table],
        axis=-1,
    )


def reverse_rotation(upstream, cosine_table, sine_table):
    half = upstream.shape[-1] // 2
    first, second = (upstream[..., :half], upstream[..., half:])
    return jnp.concatenate(
        [first * cosine_table + second * sine_table, second * cosine_table - first * sine_table],
        axis=-1,
    )


def rms_parts(field):
    inverse = lax.rsqrt(jnp.mean(field * field, axis=-1, keepdims=True) + epsilon)
    return (field * inverse, inverse)


def rms_back(upstream, normed, inverse):
    return inverse * (upstream - normed * jnp.mean(upstream * normed, axis=-1, keepdims=True))


def dot(left, right, dims, out=F32):
    got = lax.dot_general(left, right, (dims, ((), ())), preferred_element_type=F32)
    return got.astype(out)


def cross_product(left, right, out=F32):
    return dot(left, right, ((0,), (0,)), out)


def against(left, right, out=F32):
    return dot(left, right, ((1,), (1,)), out)


class Plane:
    def __init__(self):
        self.c, self.r, self.z = (lax.axis_size(a) for a in ("ctx", "rep", "fsdp"))
        self.size = self.c * self.r
        self.cube = self.c == 2 and self.r == 4 and self.z == 4
        rep = lax.axis_index("rep")
        self.y, self.x, self.core = lax.axis_index("ctx"), rep // 2, rep % 2
        self.rank = lax.axis_index("ctx") * self.r + rep
        self.layer = lax.axis_index("fsdp")
        self.place = jnp.stack([self.rank, self.layer]).astype(jnp.int32)

    def over_x(self, v):
        return lax.ppermute(v, "rep", [(i, i ^ 2) for i in range(4)])

    def over_core(self, v):
        return lax.ppermute(v, "rep", [(i, i ^ 1) for i in range(4)])

    def over_y(self, v):
        return lax.ppermute(v, "ctx", [(0, 1), (1, 0)])

    def gather_pair(self, v):
        half = v.shape[0] // 2
        from_x, from_y = self.over_x(v), self.over_y(v)
        far_a = self.over_y(from_x[:half])
        far_b = self.over_x(from_y[half:])
        near = jnp.concatenate([v, from_x, from_y, far_a, far_b], axis=0)
        other = self.over_core(near)
        shape = (4,) + v.shape
        return near.reshape(shape), other.reshape(shape)

    def gather_rows(self, v):
        if not self.cube:
            return lax.all_gather(v, PLANE, axis=0, tiled=True)
        near, other = self.gather_pair(v)
        return jnp.concatenate([near, other], axis=0).reshape(8 * v.shape[0], *v.shape[1:])

    def scatter_rows(self, v):
        if not self.cube:
            return lax.psum_scatter(v.astype(BF), PLANE, scatter_dimension=0, tiled=True).astype(F32)
        n = v.shape[0] // 8
        got = self.over_core(v[4 * n :].astype(BF)).astype(F32)
        part = lambda k: v[k * n : (k + 1) * n].astype(F32) + got[k * n : (k + 1) * n]
        return self.scatter_four(part(0), part(1), part(2), part(3))

    def scatter_four(self, mine, near_x, near_y, far):
        far = far.astype(BF)
        half = far.shape[0] // 2
        got_x, got_y = self.over_x(far[:half]), self.over_y(far[half:])
        near_y = jnp.concatenate([near_y[:half] + got_x.astype(F32), near_y[half:]], axis=0)
        near_x = jnp.concatenate([near_x[:half], near_x[half:] + got_y.astype(F32)], axis=0)
        in_x, in_y = self.over_x(near_x.astype(BF)), self.over_y(near_y.astype(BF))
        return mine + in_x.astype(F32) + in_y.astype(F32)

    def scatter(self, v):
        if not self.cube:
            moved = jnp.moveaxis(v, 1, 0)
            return lax.psum_scatter(moved.astype(BF), PLANE, scatter_dimension=0, tiled=False).astype(F32)
        v = v.reshape(v.shape[:1] + (2, 2, 2) + v.shape[2:])
        pick = lambda a, i, ax: lax.dynamic_index_in_dim(a, i, ax, keepdims=False)
        x, y, core = self.x, self.y, self.core
        got = self.over_core(pick(v, 1 - core, 3).astype(BF))
        v = pick(v, core, 3).astype(F32) + got.astype(F32)
        row, away = pick(v, y, 1), pick(v, 1 - y, 1)
        return self.scatter_four(pick(row, x, 1), pick(row, 1 - x, 1), pick(away, x, 1), pick(away, 1 - x, 1))

    def to_ranks(self, v):
        if not self.cube:
            return v
        n = v.shape[0] // 8
        v = v.reshape((2, 2, 2, n) + v.shape[1:])
        for axis, bit in ((1, self.y), (2, self.x), (0, self.core)):
            v = jnp.where(bit == 1, jnp.flip(v, axis), v)
        return jnp.moveaxis(v, 0, 2).reshape((8 * n,) + v.shape[4:])

    def from_ranks(self, v):
        if not self.cube:
            return v
        n = v.shape[0] // 8
        v = jnp.moveaxis(v.reshape((2, 2, 2, n) + v.shape[1:]), 2, 0)
        for axis, bit in ((1, self.y), (2, self.x), (0, self.core)):
            v = jnp.where(bit == 1, jnp.flip(v, axis), v)
        return v.reshape((8 * n,) + v.shape[4:])

    def exchange(self, v):
        return lax.all_to_all(v, PLANE, split_axis=0, concat_axis=0, tiled=True)

    def total(self, v):
        if not self.cube:
            return lax.psum(v, ("ctx", "fsdp", "rep"))
        v = v + self.over_core(v)
        v = v + self.over_x(v)
        v = v + self.over_y(v)
        for part in self.from_layers(lambda d: v):
            v = v + part
        return v

    def from_layers(self, get):
        z = self.z
        return [lax.ppermute(get(d), "fsdp", [(i, (i + d) % z) for i in range(z)]) for d in range(1, z)]

    def layers_gather(self, v):
        return jnp.stack([v] + self.from_layers(lambda d: v))

    def layers_scatter(self, v):
        pick = lambda d: lax.dynamic_index_in_dim(v, (self.layer + d) % self.z, 0, keepdims=False)
        total = pick(0).astype(F32)
        for part in self.from_layers(lambda d: pick(d).astype(BF)):
            total = total + part.astype(F32)
        return total


def call(body, place, arrays, grid, in_specs, out_shape, out_specs, name, **more):
    size = sum(math.prod(a.shape) * a.dtype.itemsize for a in arrays)
    return pl.pallas_call(
        body,
        out_shape=out_shape,
        grid_spec=pltpu.PrefetchScalarGridSpec(
            num_scalar_prefetch=1, grid=grid, in_specs=in_specs, out_specs=out_specs
        ),
        cost_estimate=pl.CostEstimate(flops=0, transcendentals=0, bytes_accessed=2 * size),
        name=name,
        **more,
    )(place, *arrays)


def layers_order(v, place):
    z = v.shape[0]

    def body(place_ref, source, out):
        out[...] = source[...]

    block = (1,) + v.shape[1:]
    return call(
        body,
        place,
        [v],
        (z,),
        [pl.BlockSpec(block, lambda d, at: (d, 0, 0))],
        jax.ShapeDtypeStruct(v.shape, v.dtype),
        pl.BlockSpec(block, lambda d, at: (lax.rem(at[1] - d + z, z), 0, 0)),
        "layers_order",
    )


def pair_order(pair, place):
    near, other = pair
    z, rows, columns = near.shape[1:]

    def body(place_ref, near_ref, other_ref, out):
        @pl.when(pl.program_id(0) == 0)
        def _():
            out[0, 0] = near_ref[0, 0]

        @pl.when(pl.program_id(0) == 1)
        def _():
            out[0, 0] = other_ref[0, 0]

    block = (1, 1, rows, columns)
    return call(
        body,
        place,
        [near, other],
        (2, 4, z),
        [
            pl.BlockSpec(block, lambda c, i, d, at: (jnp.where(c == 0, i, 3), jnp.where(c == 0, d, z - 1), 0, 0)),
            pl.BlockSpec(block, lambda c, i, d, at: (jnp.where(c == 1, i, 0), jnp.where(c == 1, d, 0), 0, 0)),
        ],
        jax.ShapeDtypeStruct((z, 8, rows, columns), near.dtype),
        pl.BlockSpec(block, lambda c, i, d, at: (lax.rem(at[1] - d + z, z), at[0] ^ (2 * i + c), 0, 0)),
        "pair_order",
    )


MAIN, REST = 128, 32


def unit_columns(matrix, place):
    rows, columns = matrix.shape
    groups = 8
    span = columns // groups // LANES
    block = 128

    def body(place_ref, *refs):
        out = refs[-1]
        lanes = lax.broadcasted_iota(jnp.int32, (block, LANES), 1) // REST
        turn = lax.rem(place_ref[0], 4)
        for side in range(2):
            rest = jnp.zeros((block, LANES), F32)
            for k in range(4):
                g = side * 4 + k
                out[:, side * 640 + k * MAIN : side * 640 + (k + 1) * MAIN] = refs[2 * g][...]
                turned = pltpu.roll(refs[2 * g + 1][...].astype(F32), lax.rem(k - turn + 4, 4) * REST, 1)
                rest = jnp.where(lanes == k, turned, rest)
            out[:, side * 640 + 4 * MAIN : (side + 1) * 640] = rest.astype(out.dtype)

    def main(g):
        return pl.BlockSpec((block, LANES), lambda i, at: (i, g * span + at[0]))

    def rest(g):
        return pl.BlockSpec((block, LANES), lambda i, at: (i, g * span + 8 + at[0] // 4))

    return call(
        body,
        place,
        [matrix] * (2 * groups),
        (rows // block,),
        [spec(g) for g in range(groups) for spec in (main, rest)],
        jax.ShapeDtypeStruct((rows, 1280), matrix.dtype),
        pl.BlockSpec((block, 1280), lambda i, at: (i, 0)),
        "unit_columns",
    )


def joint_columns_of(matrix, place):
    rows, columns = matrix.shape
    last = columns // LANES - 1
    block = 256

    def body(place_ref, left, right, out):
        out[:, :LANES] = left[...]
        out[:, LANES:] = right[...]

    return call(
        body,
        place,
        [matrix, matrix],
        (rows // block,),
        [
            pl.BlockSpec((block, LANES), lambda i, at: (i, 2 * at[0])),
            pl.BlockSpec((block, LANES), lambda i, at: (i, jnp.minimum(2 * at[0] + 1, last))),
        ],
        jax.ShapeDtypeStruct((rows, 2 * LANES), matrix.dtype),
        pl.BlockSpec((block, 2 * LANES), lambda i, at: (i, 0)),
        "joint_columns",
    )


def unit_merge(pair, place, side, into):
    rows = pair[0].shape[1]
    block = 64

    def body(place_ref, near, other, *refs):
        out = refs[-1]
        rank = place_ref[0]
        lanes = lax.broadcasted_iota(jnp.int32, (block, LANES), 1) // REST

        def fill(even, odd):
            def piece(k, start):
                source = odd if k % 2 else even
                index = lax.shift_right_logical(jnp.bitwise_xor(rank, k), 1)
                return source[index, :, start : start + LANES].astype(F32)

            for k in range(8):
                for g in range(4):
                    start = g * 1280 + k * MAIN
                    out[:, start : start + MAIN] = piece(k, g * MAIN)
            for b in range(2):
                rests = [piece(4 * b + q, 4 * MAIN) for q in range(4)]
                for g in range(4):
                    total = jnp.zeros((block, LANES), F32)
                    for q in range(4):
                        turned = rests[q] if q == g else pltpu.roll(rests[q], (q - g) % 4 * REST, 1)
                        total = jnp.where(lanes == q, turned, total)
                    start = g * 1280 + 8 * MAIN + b * LANES
                    out[:, start : start + LANES] = total

        @pl.when(lax.rem(rank, 2) == 0)
        def _():
            fill(near, other)

        @pl.when(lax.rem(rank, 2) == 1)
        def _():
            fill(other, near)

    source = pl.BlockSpec((4, block, 640), lambda i, at: (0, i, 0))
    arrays, specs, more = list(pair), [source, source], {}
    if into is not None:
        arrays.append(into)
        specs.append(pl.BlockSpec(memory_space=pl.ANY))
        more["input_output_aliases"] = {3: 0}
    return call(
        body,
        place,
        arrays,
        (rows // block,),
        specs,
        jax.ShapeDtypeStruct((rows, 10240), F32),
        pl.BlockSpec((block, 5120), lambda i, at: (i, side)),
        "unit_merge",
        **more,
    )


def unit_rows_merge(pair, place):
    near, other = pair
    columns = near.shape[2]
    steps = (MAIN + REST) // REST

    def body(place_ref, near_ref, other_ref, out):
        @pl.when(pl.program_id(0) == 0)
        def _():
            out[...] = near_ref[0].astype(F32)

        @pl.when(pl.program_id(0) == 1)
        def _():
            out[...] = other_ref[0].astype(F32)

    block = (1, REST, columns)

    def target(c, i, b, at):
        rank = at[0] ^ (2 * i + c)
        return (jnp.where(b < 4, 4 * rank + b, 32 + rank), 0)

    return call(
        body,
        place,
        [near, other],
        (2, 4, steps),
        [
            pl.BlockSpec(block, lambda c, i, b, at: (jnp.where(c == 0, i, 3), jnp.where(c == 0, b, steps - 1), 0)),
            pl.BlockSpec(block, lambda c, i, b, at: (jnp.where(c == 1, i, 0), jnp.where(c == 1, b, 0), 0)),
        ],
        jax.ShapeDtypeStruct((8 * (MAIN + REST), columns), F32),
        pl.BlockSpec((REST, columns), target),
        "unit_rows_merge",
    )


def rows_merge(pair, place):
    near, other = pair
    rows, columns = near.shape[1:]

    def body(place_ref, near_ref, other_ref, out):
        @pl.when(pl.program_id(0) == 0)
        def _():
            out[...] = near_ref[0].astype(F32)

        @pl.when(pl.program_id(0) == 1)
        def _():
            out[...] = other_ref[0].astype(F32)

    block = (1, rows, columns)
    return call(
        body,
        place,
        [near, other],
        (2, 4),
        [
            pl.BlockSpec(block, lambda c, i, at: (jnp.where(c == 0, i, 3), 0, 0)),
            pl.BlockSpec(block, lambda c, i, at: (jnp.where(c == 1, i, 0), 0, 0)),
        ],
        jax.ShapeDtypeStruct((8 * rows, columns), F32),
        pl.BlockSpec((rows, columns), lambda c, i, at: (at[0] ^ (2 * i + c), 0)),
        "rows_merge",
    )


def joint_merge(pair, place, columns):
    near, other = pair
    rows = near.shape[1]
    block = 128

    def body(place_ref, near_ref, other_ref, out):
        rank = place_ref[0]

        def fill(even, odd):
            for k in range(8):
                source = odd if k % 2 else even
                index = lax.shift_right_logical(jnp.bitwise_xor(rank, k), 1)
                width = min(256, columns - 256 * k)
                out[:, 256 * k : 256 * k + width] = source[index, :, :width].astype(F32)

        @pl.when(lax.rem(rank, 2) == 0)
        def _():
            fill(near_ref, other_ref)

        @pl.when(lax.rem(rank, 2) == 1)
        def _():
            fill(other_ref, near_ref)

    source = pl.BlockSpec((4, block, 256), lambda i, at: (0, i, 0))
    return call(
        body,
        place,
        [near, other],
        (rows // block,),
        [source, source],
        jax.ShapeDtypeStruct((rows, columns), F32),
        pl.BlockSpec((block, columns), lambda i, at: (i, 0)),
        "joint_merge",
    )


def after(value, *earlier):
    return lax.optimization_barrier((value, *earlier))[0]


def shards(
    tokens,
    cotangent,
    lengths,
    first_gain,
    joint_matrix,
    query_gain,
    key_gain,
    out_weight,
    second_gain,
    expand_weight,
    contract_weight,
):
    plane = Plane()
    cube, members, layers, rank, at_place = plane.cube, plane.size, plane.z, plane.rank, plane.place
    rows_here = tokens.shape[1]
    model = tokens.shape[2]
    place_ctx = lax.axis_index("ctx")
    contexts = lax.axis_size("ctx")
    span = rows_here * contexts
    slot_length_value = lengths[0]
    positions = place_ctx * rows_here + jnp.arange(rows_here, dtype=jnp.int32)
    valid = (positions < slot_length_value).astype(F32)[:, None]
    query_width = QUERY_HEADS * HEAD_SIZE
    key_width = KEY_VALUE_HEADS * HEAD_SIZE
    head_group = QUERY_HEADS // KEY_VALUE_HEADS
    scale = HEAD_SIZE ** (-0.5)
    joint_columns = joint_matrix.shape[1]

    rows = tokens[0].astype(F32)
    tokens_all = plane.gather_rows(tokens[0])

    sizes = [first_gain.shape[0], second_gain.shape[0], query_gain.shape[0], key_gain.shape[0]]
    joint_width = 2048 // members
    if cube:
        joint_share = joint_columns_of(joint_matrix, at_place)
    else:
        padded = jnp.pad(joint_matrix, ((0, 0), (0, joint_width * members - joint_columns)))
        joint_share = lax.dynamic_slice_in_dim(padded, rank * joint_width, joint_width, 1)
    packed = jnp.concatenate([first_gain, second_gain, query_gain, key_gain])
    fill = -packed.shape[0] % (8 * joint_width)
    packed = jnp.pad(packed, (0, fill)).reshape(-1, joint_width)
    joint_sent = jnp.concatenate([joint_share, packed], axis=0)
    if cube:
        joint_got = layers_order(plane.layers_gather(joint_sent), at_place)
    else:
        joint_got = lax.all_gather(joint_sent, "fsdp", axis=0, tiled=False)
    joint_rows = joint_share.shape[0]
    joint_part = joint_got[:, :joint_rows].reshape(model, joint_width)
    packed = joint_got[:, joint_rows:].reshape(layers, -1)
    gains, at = [], 0
    for size in sizes:
        gains.append(packed[:, at : at + size].reshape(-1).astype(F32))
        at += size
    gain_one, gain_two, query_scale, key_scale = gains

    out_rows = out_weight.shape[0] // members
    out_share = lax.dynamic_slice_in_dim(out_weight, rank * out_rows, out_rows, 0)
    if cube:
        out_share = after(out_share, joint_got)
        out_full = pair_order(plane.gather_pair(plane.layers_gather(out_share)), at_place)
        out_full = out_full.reshape(query_width, model)
    else:
        out_full = lax.all_gather(out_weight, "fsdp", axis=0, tiled=True)

    units = contract_weight.shape[0] // members
    width = units * layers
    if cube:
        expand_share = unit_columns(after(expand_weight, joint_sent), at_place)
        main_share = lax.dynamic_slice_in_dim(contract_weight, rank * MAIN, MAIN, 0)
        rest_share = lax.dynamic_slice_in_dim(contract_weight, members * MAIN + rank * REST, REST, 0)
        contract_share = jnp.concatenate([main_share, rest_share], axis=0)
    else:
        share = expand_weight.reshape(-1, 2 * layers, members, units)
        expand_share = lax.dynamic_index_in_dim(share, rank, 2, keepdims=False).reshape(-1, 2 * width)
        contract_share = lax.dynamic_slice_in_dim(contract_weight, rank * units, units, 0)
    expand_part = lax.all_gather(expand_share, "fsdp", axis=0, tiled=True)
    contract_part = lax.all_gather(contract_share, "fsdp", axis=0, tiled=False)
    if cube:
        contract_part = jnp.concatenate(
            [contract_part[:, :MAIN].reshape(-1, model), contract_part[:, MAIN:].reshape(-1, model)], axis=0
        )
    else:
        contract_part = contract_part.reshape(width, model)

    upstream = cotangent[0].astype(F32) * valid
    upstream_all = plane.gather_rows(after(upstream.astype(BF), tokens_all))

    entry_one_all = (rms_parts(tokens_all.astype(F32))[0] * gain_one).astype(BF)
    normed_one, inverse_one = rms_parts(rows)
    joint_columns_all = plane.to_ranks(dot(entry_one_all, joint_part, ((1,), (0,))))
    joint_projection = plane.exchange(joint_columns_all).reshape(members, rows_here, joint_width)
    joint_projection = jnp.swapaxes(joint_projection, 0, 1).reshape(rows_here, members * joint_width)
    query_raw = joint_projection[:, :query_width].reshape(rows_here, QUERY_HEADS, HEAD_SIZE)
    key_raw = joint_projection[:, query_width : query_width + key_width].reshape(
        rows_here, KEY_VALUE_HEADS, HEAD_SIZE
    )
    value_part = joint_projection[:, query_width + key_width : joint_columns]
    cosine_table, sine_table = tables(positions, HEAD_SIZE)
    query_normed, query_inverse = rms_parts(query_raw)
    rotated_query = rotate(query_normed * query_scale, cosine_table, sine_table).astype(BF)
    key_normed, key_inverse = rms_parts(key_raw)
    key_rot = rotate(key_normed * key_scale, cosine_table, sine_table).astype(BF)
    local_pair = jnp.concatenate([key_rot.reshape(rows_here, key_width), value_part.astype(BF)], axis=1)
    if contexts == 2:
        earlier = lax.ppermute(local_pair, "ctx", [(0, 1)])
        first = place_ctx == 0
        pair_all = jnp.concatenate(
            [jnp.where(first, local_pair, earlier), jnp.where(first, 0, local_pair).astype(BF)], axis=0
        )
    else:
        pair_all = lax.all_gather(local_pair, "ctx", axis=0, tiled=True)
    key_all = pair_all[:, :key_width].reshape(span, KEY_VALUE_HEADS, HEAD_SIZE)
    value_all = pair_all[:, key_width:].reshape(span, KEY_VALUE_HEADS, HEAD_SIZE)
    grouped_query = rotated_query.reshape(rows_here, KEY_VALUE_HEADS, head_group, HEAD_SIZE)
    key_pos = jnp.arange(span, dtype=jnp.int32)
    allowed = (key_pos[None, :] <= positions[:, None]) & (key_pos[None, :] < slot_length_value)
    scores = jnp.einsum("qgrd,kgd->grqk", grouped_query, key_all, preferred_element_type=F32) * scale
    scores = jnp.where(allowed, scores, masked_fill_value)
    powers = jnp.where(allowed, jnp.exp(scores - jnp.max(scores, axis=-1, keepdims=True)), 0.0)
    shares = powers / jnp.sum(powers, axis=-1, keepdims=True)
    shares_b = shares.astype(BF)
    mixed = jnp.einsum("grqk,kgd->qgrd", shares_b, value_all, preferred_element_type=F32)
    mixed_output = mixed.reshape(rows_here, query_width).astype(BF)
    hidden = rows + dot(mixed_output, out_full, ((1,), (0,)))

    normed_two, inverse_two = rms_parts(hidden)
    entry_two = (normed_two * gain_two).astype(BF)
    entry_all = plane.gather_rows(entry_two)
    expanded = dot(entry_all, expand_part, ((1,), (0,)))
    gate, upward = expanded[:, :width], expanded[:, width:]
    sigma = jax.nn.sigmoid(gate)
    activated = gate * sigma
    product = (activated * upward).astype(BF)
    contract_grad = cross_product(product, upstream_all, BF)
    if cube:
        contract_grad = jnp.concatenate(
            [
                contract_grad[: layers * MAIN].reshape(layers, MAIN, model),
                contract_grad[layers * MAIN :].reshape(layers, REST, model),
            ],
            axis=1,
        )
    else:
        contract_grad = contract_grad.reshape(layers, units, model)
    contract_owned = lax.psum_scatter(contract_grad, "fsdp", scatter_dimension=0, tiled=False)
    back_product = against(upstream_all, contract_part)
    grad_gate = (back_product * upward * sigma * (1.0 + gate * (1.0 - sigma))).astype(BF)
    grad_upward = (back_product * activated).astype(BF)
    grad_expanded = jnp.concatenate([grad_gate, grad_upward], axis=1)
    back_entry_two = plane.scatter_rows(against(grad_expanded, expand_part))
    gate_grad = cross_product(entry_all, grad_gate, BF)
    up_grad = cross_product(entry_all, grad_upward, BF)
    gate_owned = lax.psum_scatter(gate_grad, "fsdp", scatter_dimension=0, tiled=True)
    up_owned = lax.psum_scatter(up_grad, "fsdp", scatter_dimension=0, tiled=True)
    branch_two = plane.scatter_rows(dot(product, contract_part, ((1,), (0,))))
    layer_output = ((hidden + branch_two) * valid).astype(BF)

    second_grad = jnp.sum(back_entry_two * normed_two, axis=0)
    back_hidden = upstream + rms_back(back_entry_two * gain_two, normed_two, inverse_two)

    back_hidden_b = back_hidden.astype(BF)
    out_grad = cross_product(mixed_output, back_hidden_b, BF)
    out_mine = plane.scatter(out_grad.reshape(layers, members, out_rows, model))
    mixed_backward = against(back_hidden_b, out_full, BF)
    group_backward = mixed_backward.reshape(rows_here, KEY_VALUE_HEADS, head_group, HEAD_SIZE)
    back_shares = jnp.einsum("qgrd,kgd->grqk", group_backward, value_all, preferred_element_type=F32)
    offset = jnp.sum(shares * back_shares, axis=-1, keepdims=True)
    back_scores = (shares * (back_shares - offset)).astype(BF)
    grad_query = jnp.einsum("grqk,kgd->qgrd", back_scores, key_all, preferred_element_type=F32)
    grad_keys = jnp.einsum("grqk,qgrd->kgd", back_scores, grouped_query, preferred_element_type=F32) * scale
    grad_values = jnp.einsum("grqk,qgrd->kgd", shares_b, group_backward, preferred_element_type=F32)
    pair_grads = jnp.concatenate(
        [grad_keys.reshape(span, key_width), grad_values.reshape(span, key_width)], axis=1
    )
    if contexts == 2:
        later = lax.ppermute(pair_grads[:rows_here], "ctx", [(1, 0)])
        pair_mine = jnp.where(first, pair_grads[:rows_here] + later, pair_grads[rows_here:])
    else:
        pair_mine = lax.psum_scatter(pair_grads, "ctx", scatter_dimension=0, tiled=True)
    back_query_rot = reverse_rotation(
        grad_query.reshape(rows_here, QUERY_HEADS, HEAD_SIZE) * scale, cosine_table, sine_table
    )
    query_gain_grad = jnp.sum(back_query_rot * query_normed, axis=(0, 1))
    grad_query_raw = rms_back(back_query_rot * query_scale, query_normed, query_inverse)
    back_key_rot = reverse_rotation(
        pair_mine[:, :key_width].reshape(rows_here, KEY_VALUE_HEADS, HEAD_SIZE), cosine_table, sine_table
    )
    key_gain_grad = jnp.sum(back_key_rot * key_normed, axis=(0, 1))
    grad_key_raw = rms_back(back_key_rot * key_scale, key_normed, key_inverse)
    grad_joint = jnp.concatenate(
        [
            grad_query_raw.reshape(rows_here, query_width),
            grad_key_raw.reshape(rows_here, key_width),
            pair_mine[:, key_width:],
            jnp.zeros((rows_here, members * joint_width - joint_columns), F32),
        ],
        axis=1,
    ).astype(BF)
    grad_joint = jnp.swapaxes(grad_joint.reshape(rows_here, members, joint_width), 0, 1)
    grad_columns = plane.from_ranks(plane.exchange(grad_joint.reshape(members * rows_here, joint_width)))
    joint_grad = cross_product(entry_one_all, grad_columns, BF).reshape(layers, -1, joint_width)
    back_entry_one = plane.scatter_rows(against(grad_columns, joint_part))
    first_grad = jnp.sum(back_entry_one * normed_one, axis=0)
    input_gradient = back_hidden + rms_back(back_entry_one * gain_one, normed_one, inverse_one)

    small = plane.total(jnp.concatenate([first_grad, second_grad, query_gain_grad, key_gain_grad]))
    out_owned = plane.layers_scatter(out_mine).astype(BF)
    joint_owned = plane.layers_scatter(joint_grad).astype(BF)
    if cube:
        contract_gradient = unit_rows_merge(plane.gather_pair(contract_owned), at_place)
        half = unit_merge(plane.gather_pair(gate_owned), at_place, 0, None)
        out_gradient = rows_merge(plane.gather_pair(out_owned), at_place)
        joint_gradient = joint_merge(plane.gather_pair(joint_owned), at_place, joint_columns)
        expand_gradient = unit_merge(plane.gather_pair(up_owned), at_place, 1, half)
    else:
        every = lambda v: lax.all_gather(v, PLANE, axis=0, tiled=False)
        contract_gradient = every(contract_owned).reshape(members * units, model).astype(F32)
        both = jnp.concatenate([every(gate_owned), every(up_owned)], axis=2)
        both = both.reshape(members, -1, 2 * layers, units).transpose(1, 2, 0, 3)
        expand_gradient = both.reshape(-1, 2 * layers * members * units).astype(F32)
        out_gradient = every(out_owned).reshape(members * out_rows, model).astype(F32)
        joint_gradient = jnp.moveaxis(every(joint_owned), 0, 1).reshape(joint_rows, -1)[:, :joint_columns].astype(F32)
    owned, at = [], 0
    for size in sizes:
        owned.append(lax.dynamic_slice_in_dim(small, at + plane.layer * size, size))
        at += size * layers
    return (
        layer_output[None],
        input_gradient[None],
        owned[0],
        joint_gradient,
        owned[2],
        owned[3],
        out_gradient,
        owned[1],
        expand_gradient,
        contract_gradient,
    )


def solution(mesh):
    return jax.shard_map(
        shards,
        mesh=mesh,
        in_specs=(
            P(("fsdp", "rep"), "ctx", None),
            P(("fsdp", "rep"), "ctx", None),
            P(("fsdp", "rep")),
            P("fsdp"),
            P("fsdp", None),
            P("fsdp"),
            P("fsdp"),
            P("fsdp", None),
            P("fsdp"),
            P("fsdp", None),
            P("fsdp", None),
        ),
        out_specs=(
            P(("fsdp", "rep"), "ctx", None),
            P(("fsdp", "rep"), "ctx", None),
            P("fsdp"),
            P("fsdp", None),
            P("fsdp"),
            P("fsdp"),
            P("fsdp", None),
            P("fsdp"),
            P("fsdp", None),
            P("fsdp", None),
        ),
        check_vma=False,
    )
```
